32 devices in a mesh: vocab: 4 (over z), expert: 8 (over y, x, core).
Axes of the slice: x: 2, y: 2, z: 4, core: 2. Of those that a mesh axis runs over, the one named last changes fastest.
Arguments:
- token_ids: int32 [1024], replicated, may hold values from 0 to 75967
- word_mask: int32 [75968], P('vocab'), may hold values 0 or 1
- embed_table: bfloat16 [75968, 4096], P('vocab', 'expert'), may hold values from -6 to 6
- attn_out: bfloat16 [1024, 4096], P('expert', 'vocab'), may hold values from -6 to 6
- in_gain: float32 [4096], replicated, may hold values from 0.25 to 1.75
- key_weight: bfloat16 [4096, 512], P(None, 'vocab'), may hold values from -0.09375 to 0.09375
- key_gain: float32 [128], replicated, may hold values from 0.25 to 1.75
- post_gain: float32 [4096], replicated, may hold values from 0.25 to 1.75
- routes: int32 [1024, 8], P('expert'), may hold values from 0 to 15, all different within a row; in each aligned block of 128 rows (0 to 127, 128 to 255, ...) at most 96 rows name the same one
- gate_ints: int32 [1024, 8], P('expert'), may hold values from 1 to 63
- w_gate: bfloat16 [32, 4096, 768], P(('expert', 'vocab')), may hold values from -0.09375 to 0.09375
- w_up: bfloat16 [32, 4096, 768], P(('expert', 'vocab')), may hold values from -0.09375 to 0.09375
- w_down: bfloat16 [32, 768, 4096], P(('expert', 'vocab')), may hold values from -0.15625 to 0.15625
Outputs:
- expert_out: bfloat16 [1024, 4096], P('expert', 'vocab')
- key_heads: bfloat16 [1024, 512], P('expert', 'vocab')
The draws below stay inside these ranges and needn't reach their ends.
Inputs may be any that keep to these rules, and one draw needn't show every extreme that they name: `routes`: each row names 8 different experts; within the 128 rows of one index of expert no expert is named by more than 96 rows, and in some such blocks one is named by exactly 96.
All inputs are finite; a program needn't handle non-finite values. No bound on the sum of `word_mask` on one device may be relied on, other than what follows from the above.
Results may differ from the reference program's by a relative error of at most 0.008.
Values may be sent and summed in bfloat16 or wider, within the bound.
A program may use at most 192 MiB of HBM per device.

```python
import math
import jax
import jax.numpy as jnp
import numpy as np
from jax import lax

D = 4096
FF = 1536
VOCAB = 75968
HD = 128
KVH = 4
TOPK = 8
TOK_DEV = 128
TOKENS = 1024
EXPERTS = 16
CAP = 96
N_EXPERT = 8


def with_ends(drawn, key, low, high):
    place = [jax.random.randint(jax.random.fold_in(key, axis), (), 0, length) for axis, length in enumerate(drawn.shape)]
    widest = drawn.shape.index(max(drawn.shape))
    next_to = place[:widest] + [(place[widest] + 1) % drawn.shape[widest]] + place[widest + 1:]
    return drawn.at[tuple(place)].set(low).at[tuple(next_to)].set(high)


def steps_of(own_key, dims, cuts, least, largest):
    loudness, own = 1.0, jax.random.fold_in(own_key, 6)
    for axis_at, parts in cuts:
        heights = jnp.exp(jax.random.uniform(jax.random.fold_in(own, axis_at), (parts,), jnp.float32, least / len(cuts), largest / len(cuts)))
        loudness = loudness * jnp.repeat(heights, dims[axis_at] // parts).reshape([-1 if axis == axis_at else 1 for axis in range(len(dims))])
    return loudness


def ranked_wide(key, extent, count, slope):
    weights = [min(1 << octave, count + 1 - (1 << octave)) * (1 << 20) // math.isqrt((1 << octave) ** slope) + 1 for octave in range((count + 1).bit_length()) if 1 << octave <= count]
    deviation = 1 + sum(weights) // (1 << 30)
    table = np.cumsum(np.array([max(1, weight // deviation) for weight in weights]))
    ticket = jax.random.randint(jax.random.fold_in(key, 1), extent, 0, int(table[len(weights) - 1]))
    start = jnp.left_shift(1, jnp.searchsorted(jnp.asarray(table, jnp.int32), ticket, side="right").astype(jnp.int32))
    rank = start - 1 + jax.random.randint(jax.random.fold_in(key, 4), extent, 0, 1 << 30) % jnp.minimum(start, count + 1 - start)
    return jax.random.permutation(jax.random.fold_in(key, 2), count)[rank].astype(jnp.int32)


def assign_block(own_key, own, number, rows, count, top, limit, skew):
    sequence = jax.random.permutation(own_key, count)
    crowded, usual = load_shares(count, rows * top, limit, skew, True), load_shares(count, rows * top, limit, skew, False)
    places = jnp.arange(count)

    def named(sizes, rotation):
        used = int((sizes > 0).sum())
        fixed = max(1, used // 4)
        passed = fixed + (places - fixed + rotation * (used - fixed)) % max(1, count - fixed)
        return jnp.zeros((count,), jnp.int32).at[sequence[jnp.where(places < fixed, places, passed)]].set(jnp.asarray(sizes, jnp.int32))

    sizes = jnp.where(number % 4 == 0, named(crowded, number // 4), named(usual, number - number // 4 - 1))
    mixed = jax.random.permutation(jax.random.fold_in(own, 3), count)
    giver, sink = mixed[0:count // 2 * 2:2], mixed[1:count // 2 * 2:2]
    room = jnp.minimum(sizes[giver] - 1, limit - sizes[sink]) // 2
    room = jnp.where((giver == sequence[0]) | (sink == sequence[0]) | (sizes[sink] == 0), 0, jnp.maximum(room, 0))
    passed = jax.random.randint(jax.random.fold_in(own, 4), (count // 2,), 0, 1 << 20) % (room + 1)
    sizes = sizes.at[giver].add(-passed).at[sink].add(passed)
    labels = jnp.searchsorted(jnp.cumsum(sizes), jnp.arange(rows * top), side="right").astype(jnp.int32)
    grid = labels.reshape(top, rows).T
    grid = grid[jax.random.permutation(jax.random.fold_in(own, 1), rows)]
    rotation = jax.random.randint(jax.random.fold_in(own, 2), (rows, 1), 0, top)
    return jnp.take_along_axis(grid, (jnp.arange(top)[None, :] + rotation) % top, axis=1)


def load_shares(amount, total, reach, slope, full):
    portions = [(1 << 20) // math.isqrt(rank ** slope) + 1 for rank in range(1, amount + 1)]
    largest = reach if full else min(reach, max(-(-total // amount), total * portions[0] // sum(portions)))
    least = 1 if total - largest >= amount - 1 else 0
    counts, rest = [largest] + [least] * (amount - 1), total - largest - least * (amount - 1)
    while rest > 0:
        candidates = [i for i in range(1, amount) if counts[i] < largest] or [i for i in range(1, amount) if counts[i] < reach]
        pool, left = sum([portions[i] for i in candidates]), rest
        for i in candidates:
            extra = min(reach - counts[i], max(1, left * portions[i] // pool), rest)
            counts[i] = counts[i] + extra
            rest = rest - extra
    return np.array(counts)


def noise(own_key, extent, deviation, reach, pieces=(), kind=jnp.bfloat16):
    loudness = steps_of(own_key, extent, pieces, -0.22, 0.18) if pieces else 1.0
    array = jax.random.normal(own_key, extent, jnp.float32) * deviation * loudness
    return jnp.minimum(jnp.maximum(array, -reach), reach).astype(kind)


def setup_inputs(seed: int = 0) -> dict:
    arg_keys = jax.random.split(jax.random.key(seed), 14)
    token_ids = with_ends(ranked_wide(arg_keys[0], (TOKENS,), VOCAB, 2), jax.random.fold_in(arg_keys[0], 3), 0, VOCAB - 1).astype(jnp.int32)
    word_mask = with_ends((jax.random.randint(arg_keys[1], (VOCAB,), 0, 4) < 3).astype(jnp.int32), jax.random.fold_in(arg_keys[1], 1), 0, 1)
    embed_table = noise(arg_keys[2], (VOCAB, D), 1.0, 6.0, ((0, 4), (1, 8)))
    attn_out = noise(arg_keys[3], (TOKENS, D), 1.0, 6.0, ((0, 8), (1, 4)))
    in_gain = jnp.clip(1.0 + 0.15 * jax.random.normal(arg_keys[4], (D,), jnp.float32), 0.25, 1.75)
    key_weight = noise(arg_keys[5], (D, KVH * HD), D ** -0.5, 0.09375, ((1, 4),))
    key_gain = jnp.clip(1.0 + 0.15 * jax.random.normal(arg_keys[6], (HD,), jnp.float32), 0.25, 1.75)
    post_gain = jnp.clip(1.0 + 0.15 * jax.random.normal(arg_keys[7], (D,), jnp.float32), 0.25, 1.75)
    routes_keys = jax.random.split(jax.random.fold_in(arg_keys[8], 1), TOKENS // TOK_DEV)
    routes_turns = jax.random.permutation(jax.random.fold_in(arg_keys[8], 3), TOKENS // TOK_DEV)
    routes = jax.vmap(lambda own, number: assign_block(jax.random.fold_in(arg_keys[8], 2), own, number, TOK_DEV, EXPERTS, TOPK, CAP, 2))(routes_keys, routes_turns).reshape((TOKENS, TOPK))
    gate_ints = with_ends(jax.random.randint(arg_keys[9], (TOKENS, TOPK), 1, 64), jax.random.fold_in(arg_keys[9], 1), 1, 63).astype(jnp.int32)
    w_gate = noise(arg_keys[10], (2 * EXPERTS, D, FF // 2), D ** -0.5, 0.09375, ((0, 32),))
    w_up = noise(arg_keys[11], (2 * EXPERTS, D, FF // 2), D ** -0.5, 0.09375, ((0, 32),))
    w_down = noise(arg_keys[12], (2 * EXPERTS, FF // 2, D), FF ** -0.5, 0.15625, ((0, 32),))
    return dict(token_ids=token_ids, word_mask=word_mask, embed_table=embed_table, attn_out=attn_out, in_gain=in_gain, key_weight=key_weight, key_gain=key_gain, post_gain=post_gain, routes=routes, gate_ints=gate_ints, w_gate=w_gate, w_up=w_up, w_down=w_down)


def rms_rows(values, scale_gain):
    inverse_rms = lax.rsqrt(lax.optimization_barrier(jnp.mean(values * values, axis=-1, keepdims=True)) + 1e-06)
    return values * inverse_rms * scale_gain

def reference(token_ids, word_mask, embed_table, attn_out, in_gain, key_weight, key_gain, post_gain, routes, gate_ints, w_gate, w_up, w_down):
    keep_row = word_mask[token_ids] == 1
    embedded = jnp.where(keep_row[:, None], embed_table[token_ids], jnp.zeros_like(embed_table[:1]))
    normed = rms_rows(embedded.astype(jnp.float32), in_gain).astype(jnp.bfloat16)
    raw_keys = jnp.dot(normed, key_weight, preferred_element_type=jnp.float32)
    head_view = raw_keys.reshape(TOKENS, KVH, HD)
    key_heads = rms_rows(head_view, key_gain).astype(jnp.bfloat16).reshape(TOKENS, KVH * HD)
    mid_stream = (embedded.astype(jnp.float32) + attn_out.astype(jnp.float32)).astype(jnp.bfloat16)
    expert_in = rms_rows(mid_stream.astype(jnp.float32), post_gain).astype(jnp.bfloat16)
    gate_share = gate_ints.astype(jnp.float32) / lax.optimization_barrier(jnp.sum(gate_ints, axis=1, keepdims=True)).astype(jnp.float32)
    blocks = routes.reshape(N_EXPERT, TOK_DEV * TOPK).astype(jnp.int32)
    onehot = (blocks[:, :, None] == jnp.arange(EXPERTS, dtype=jnp.int32)[None, None, :]).astype(jnp.int32)
    slot_rank = lax.optimization_barrier(jnp.sum((jnp.cumsum(onehot, axis=1).astype(jnp.int32) - onehot) * onehot, axis=2)).astype(jnp.int32)
    block_ids = jnp.arange(N_EXPERT, dtype=jnp.int32)[:, None]
    assign_ids = jnp.arange(TOK_DEV * TOPK, dtype=jnp.int32)[None, :]
    token_of = (block_ids * TOK_DEV + assign_ids // TOPK).astype(jnp.int32)
    slot_index = ((blocks * N_EXPERT + block_ids) * CAP + slot_rank).astype(jnp.int32)
    slot_token = jnp.full((EXPERTS * N_EXPERT * CAP,), TOKENS, jnp.int32).at[slot_index.reshape(-1)].set(token_of.reshape(-1))
    slot_gate = jnp.zeros((EXPERTS * N_EXPERT * CAP,), jnp.float32).at[slot_index.reshape(-1)].set(gate_share.reshape(-1))
    padded_in = jnp.concatenate([expert_in, jnp.zeros((1, D), expert_in.dtype)], axis=0)

    def one_expert(expert, running):
        token_list = lax.dynamic_slice_in_dim(slot_token, expert * N_EXPERT * CAP, N_EXPERT * CAP)
        gate_list = lax.dynamic_slice_in_dim(slot_gate, expert * N_EXPERT * CAP, N_EXPERT * CAP)
        row_block = padded_in[jnp.clip(token_list, 0, TOKENS)]
        summed_parts = jnp.zeros((N_EXPERT * CAP, D), jnp.float32)
        for part_idx in range(2):
            entry_idx = 2 * expert + part_idx
            gate_mat = lax.dynamic_index_in_dim(w_gate, entry_idx, 0, keepdims=False)
            up_mat = lax.dynamic_index_in_dim(w_up, entry_idx, 0, keepdims=False)
            down_mat = lax.dynamic_index_in_dim(w_down, entry_idx, 0, keepdims=False)
            gate_val = jnp.dot(row_block, gate_mat, preferred_element_type=jnp.float32)
            up_val = jnp.dot(row_block, up_mat, preferred_element_type=jnp.float32)
            hidden = (jax.nn.silu(gate_val) * up_val).astype(jnp.bfloat16)
            summed_parts = summed_parts + jnp.dot(hidden, down_mat, preferred_element_type=jnp.float32)
        part_rows = lax.optimization_barrier(summed_parts.astype(jnp.bfloat16)).astype(jnp.float32)
        return running.at[token_list].add(gate_list[:, None] * part_rows, mode='drop')
    running = lax.fori_loop(0, EXPERTS, one_expert, jnp.zeros((TOKENS, D), jnp.float32))
    return (running.astype(jnp.bfloat16), key_heads)
```

```python
import jax
import jax.numpy as jnp
from jax import lax
from jax.sharding import PartitionSpec as P


def rms_rows(values, scale_gain):
    inverse_rms = lax.rsqrt(jnp.mean(values * values, axis=-1, keepdims=True) + 1e-06)
    return values * inverse_rms * scale_gain


def on_device(
    token_ids,
    word_mask,
    embed_table,
    attn_out,
    in_gain,
    key_weight,
    key_gain,
    post_gain,
    routes,
    gate_ints,
    w_gate,
    w_up,
    w_down,
):
    n_vocab = lax.axis_size("vocab")
    n_expert = lax.axis_size("expert")
    vocab_rows = embed_table.shape[0]
    experts_total = n_expert * n_vocab // 2
    whole_mesh = ("expert", "vocab")
    my_vocab = lax.axis_index("vocab")
    my_expert = (lax.axis_index("expert") * n_vocab + my_vocab) // 2

    gate_share = gate_ints.astype(jnp.float32) / jnp.sum(gate_ints, axis=1, keepdims=True).astype(
        jnp.float32
    )
    onehot = routes[:, :, None] == jnp.arange(experts_total, dtype=jnp.int32)[None, None, :]
    share_of = jnp.sum(jnp.where(onehot, gate_share[:, :, None], 0.0), axis=1)
    all_shares = lax.all_gather(share_of, "expert", axis=0, tiled=True)
    my_share = lax.dynamic_slice_in_dim(all_shares, my_expert, 1, axis=1)

    attn_rows = lax.all_to_all(attn_out, "vocab", split_axis=0, concat_axis=1, tiled=True)

    local_ids = token_ids - my_vocab * vocab_rows
    inside = (local_ids >= 0) & (local_ids < vocab_rows)
    safe_ids = jnp.clip(local_ids, 0, vocab_rows - 1)
    keep_row = inside & (word_mask[safe_ids] == 1)
    partial_value = jnp.where(
        keep_row[:, None], embed_table[safe_ids], jnp.zeros_like(embed_table[:1])
    )
    moved_rows = lax.all_to_all(partial_value, "expert", split_axis=0, concat_axis=1, tiled=True)
    rows = lax.psum_scatter(moved_rows, "vocab", scatter_dimension=0, tiled=True)
    rows = rows.astype(jnp.float32)

    mid_rows = (rows + attn_rows.astype(jnp.float32)).astype(jnp.bfloat16)
    expert_in = rms_rows(mid_rows.astype(jnp.float32), post_gain).astype(jnp.bfloat16)
    tokens_in = lax.all_gather(expert_in, whole_mesh, axis=0, tiled=True)

    normed_rows = rms_rows(rows, in_gain).astype(jnp.bfloat16)
    key_rows = lax.all_gather(normed_rows, "vocab", axis=0, tiled=True)
    raw_keys = jnp.dot(key_rows, key_weight, preferred_element_type=jnp.float32)
    key_heads = rms_rows(raw_keys, key_gain).astype(jnp.bfloat16)

    gate_val = jnp.dot(tokens_in, w_gate[0], preferred_element_type=jnp.float32)
    up_val = jnp.dot(tokens_in, w_up[0], preferred_element_type=jnp.float32)
    hidden = (jax.nn.silu(gate_val) * up_val).astype(jnp.bfloat16)
    parts = jnp.dot(hidden, w_down[0], preferred_element_type=jnp.float32)
    weighted = (parts * my_share).astype(jnp.bfloat16)
    by_tokens = lax.psum_scatter(weighted, "expert", scatter_dimension=0, tiled=True)
    expert_out = lax.psum_scatter(by_tokens, "vocab", scatter_dimension=1, tiled=True)
    return (expert_out, key_heads)


def solution(mesh):
    return jax.shard_map(
        on_device,
        mesh=mesh,
        in_specs=(
            P(),
            P("vocab"),
            P("vocab", "expert"),
            P("expert", "vocab"),
            P(),
            P(None, "vocab"),
            P(),
            P(),
            P("expert", None),
            P("expert", None),
            P(("expert", "vocab"), None, None),
            P(("expert", "vocab"), None, None),
            P(("expert", "vocab"), None, None),
        ),
        out_specs=(P("expert", "vocab"), P("expert", "vocab")),
        check_vma=False,
    )
```

```python
import jax
import jax.numpy as jnp
from jax import lax
from jax.sharding import PartitionSpec as P


def rms_rows(values, scale_gain):
    inverse_rms = lax.rsqrt(jnp.mean(values * values, axis=-1, keepdims=True) + 1e-06)
    return values * inverse_rms * scale_gain


def on_device(
    token_ids,
    word_mask,
    embed_table,
    attn_out,
    in_gain,
    key_weight,
    key_gain,
    post_gain,
    routes,
    gate_ints,
    w_gate,
    w_up,
    w_down,
):
    n_vocab = lax.axis_size("vocab")
    n_expert = lax.axis_size("expert")
    vocab_rows = embed_table.shape[0]
    experts_total = n_expert * n_vocab // 2
    whole_mesh = ("expert", "vocab")
    my_vocab = lax.axis_index("vocab")
    my_expert = (lax.axis_index("expert") * n_vocab + my_vocab) // 2

    gate_share = gate_ints.astype(jnp.float32) / jnp.sum(gate_ints, axis=1, keepdims=True).astype(
        jnp.float32
    )
    onehot = routes[:, :, None] == jnp.arange(experts_total, dtype=jnp.int32)[None, None, :]
    share_of = jnp.sum(jnp.where(onehot, gate_share[:, :, None], 0.0), axis=1)
    all_shares = lax.all_gather(share_of, "expert", axis=0, tiled=True)
    my_share = lax.dynamic_slice_in_dim(all_shares, my_expert, 1, axis=1)

    own_rows = attn_out.shape[0] // n_vocab
    attn_full = lax.all_gather(attn_out, "vocab", axis=1, tiled=True)
    attn_rows = lax.dynamic_slice_in_dim(attn_full, my_vocab * own_rows, own_rows, axis=0)

    local_ids = token_ids - my_vocab * vocab_rows
    inside = (local_ids >= 0) & (local_ids < vocab_rows)
    safe_ids = jnp.clip(local_ids, 0, vocab_rows - 1)
    keep_row = inside & (word_mask[safe_ids] == 1)
    partial_value = jnp.where(
        keep_row[:, None], embed_table[safe_ids], jnp.zeros_like(embed_table[:1])
    )
    moved_rows = lax.all_to_all(partial_value, "expert", split_axis=0, concat_axis=1, tiled=True)
    rows = lax.psum_scatter(moved_rows, "vocab", scatter_dimension=0, tiled=True)
    rows = rows.astype(jnp.float32)

    mid_rows = (rows + attn_rows.astype(jnp.float32)).astype(jnp.bfloat16)
    expert_in = rms_rows(mid_rows.astype(jnp.float32), post_gain).astype(jnp.bfloat16)
    tokens_in = lax.all_gather(expert_in, whole_mesh, axis=0, tiled=True)

    normed_rows = rms_rows(rows, in_gain).astype(jnp.bfloat16)
    tokens_in, normed_rows = lax.optimization_barrier((tokens_in, normed_rows))
    key_rows = lax.all_gather(normed_rows, "vocab", axis=0, tiled=True)
    gate_val = jnp.dot(tokens_in, w_gate[0], preferred_element_type=jnp.float32)
    up_val = jnp.dot(tokens_in, w_up[0], preferred_element_type=jnp.float32)
    hidden = (jax.nn.silu(gate_val) * up_val).astype(jnp.bfloat16)
    parts = jnp.dot(hidden, w_down[0], preferred_element_type=jnp.float32)
    weighted = (parts * my_share).astype(jnp.bfloat16)
    weighted, key_rows = lax.optimization_barrier((weighted, key_rows))
    raw_keys = jnp.dot(key_rows, key_weight, preferred_element_type=jnp.float32)
    key_heads = rms_rows(raw_keys, key_gain).astype(jnp.bfloat16)
    by_tokens = lax.psum_scatter(weighted, "expert", scatter_dimension=0, tiled=True)
    expert_out = lax.psum_scatter(by_tokens, "vocab", scatter_dimension=1, tiled=True)
    return (expert_out, key_heads)


def solution(mesh):
    return jax.shard_map(
        on_device,
        mesh=mesh,
        in_specs=(
            P(),
            P("vocab"),
            P("vocab", "expert"),
            P("expert", "vocab"),
            P(),
            P(None, "vocab"),
            P(),
            P(),
            P("expert", None),
            P("expert", None),
            P(("expert", "vocab"), None, None),
            P(("expert", "vocab"), None, None),
            P(("expert", "vocab"), None, None),
        ),
        out_specs=(P("expert", "vocab"), P("expert", "vocab")),
        check_vma=False,
    )
```

```python
import jax
import jax.numpy as jnp
from jax import lax
from jax.experimental import pallas as pl
from jax.experimental.pallas import tpu as pltpu
from jax.sharding import PartitionSpec as P


def rms_rows(values, scale_gain):
    inverse_rms = lax.rsqrt(jnp.mean(values * values, axis=-1, keepdims=True) + 1e-06)
    return values * inverse_rms * scale_gain


def greet(peers):
    barrier = pltpu.get_barrier_semaphore()
    for peer in peers:
        pl.semaphore_signal(barrier, inc=1, device_id=peer, device_id_type=pl.DeviceIdType.MESH)
    pl.semaphore_wait(barrier, len(peers))


def peers_of(n_vocab):
    me = lax.axis_index("expert")
    z = lax.axis_index("vocab")
    core, x, y = me % 2, (me // 2) % 2, me // 4
    sib, xn, yn = me + 1 - 2 * core, me + 2 - 4 * x, me + 4 - 8 * y
    along_z = [(z + d) % n_vocab for d in range(1, n_vocab)]
    ids = [{"expert": sib}, {"expert": xn}, {"expert": yn}] + [{"vocab": p} for p in along_z]
    return me, z, core, x, y, sib, xn, yn, along_z, ids


def add_rows(dst, terms):
    def step(i, carry):
        rows = pl.ds(pl.multiple_of(i * 16, 16), 16)
        total = terms[0][rows, :].astype(jnp.float32)
        for term in terms[1:]:
            total = total + term[rows, :].astype(jnp.float32)
        dst[rows, :] = total.astype(dst.dtype)
        return carry

    lax.fori_loop(0, dst.shape[0] // 16, step, 0)


def reduce_kernel(n_vocab, w, out, core_in, mine, held, a_in, b_in, a_last, b_last, full, z_in,
                  send, recv, local):
    me, z, core, x, y, sib, xn, yn, along_z, ids = peers_of(n_vocab)
    greet(ids)
    to_sib, to_x, to_y = ids[:3]
    chunk = [(1 - y) * 2 + 1 - x, y * 2 + 1 - x, (1 - y) * 2 + x, y * 2 + x]

    def move(src, dst, at, peer):
        return pltpu.make_async_remote_copy(
            src_ref=src, dst_ref=dst, send_sem=send.at[at], recv_sem=recv.at[at],
            device_id=peer, device_id_type=pl.DeviceIdType.MESH)

    core_moves = [move(w.at[chunk[r], 1 - core], core_in.at[r], r, to_sib) for r in range(4)]
    own = [pltpu.make_async_copy(w.at[chunk[r], core], mine.at[r], local.at[r]) for r in range(4)]
    for r in range(4):
        core_moves[r].start()
        own[r].start()
    a_moves = [move(held.at[0, 0], a_in.at[0], 4, to_x), move(held.at[1, 0], a_in.at[1], 5, to_x)]
    b_moves = [move(held.at[0, 1], b_in.at[0], 6, to_y), move(held.at[2, 1], b_in.at[1], 7, to_y)]
    a_then = move(held.at[2, 0], a_last, 8, to_y)
    b_then = move(held.at[1, 1], b_last, 9, to_x)
    half = held.shape[3]
    for r in range(4):
        own[r].wait()
        core_moves[r].wait_recv()
        for h in range(2):
            columns = pl.ds(h * half, half)
            add_rows(held.at[r, h], [mine.at[r, :, columns], core_in.at[r, :, columns]])
        if r == 0:
            a_moves[0].start()
            b_moves[0].start()
        if r == 1:
            a_moves[1].start()
        if r == 2:
            b_moves[1].start()
    a_moves[0].wait_recv()
    add_rows(held.at[2, 0], [held.at[2, 0], a_in.at[0]])
    a_then.start()
    b_moves[0].wait_recv()
    add_rows(held.at[1, 1], [held.at[1, 1], b_in.at[0]])
    b_then.start()
    quarter = full.shape[2]
    per_half = half // quarter
    for moves, then, came, last, h in ((a_moves, a_then, a_in, a_last, 0),
                                       (b_moves, b_then, b_in, b_last, 1)):
        moves[1].wait_recv()
        then.wait_recv()
        for q in range(per_half):
            columns = pl.ds(q * quarter, quarter)
            add_rows(full.at[h * per_half + q],
                     [held.at[3, h, :, columns], came.at[1, :, columns], last.at[:, columns]])
    z_moves = [move(full.at[along_z[d]], z_in.at[d], 10 + d, {"vocab": along_z[d]})
               for d in range(n_vocab - 1)]
    for moved in z_moves:
        moved.start()
    for moved in z_moves:
        moved.wait_recv()
    add_rows(out, [full.at[z]] + [z_in.at[d] for d in range(n_vocab - 1)])
    for moved in core_moves + a_moves + b_moves + [a_then, b_then] + z_moves:
        moved.wait_send()


def reduce_to_owners(weighted, n_vocab):
    tokens, width = weighted.shape
    rows, half, quarter = tokens // 8, width // 2, width // n_vocab
    kind = weighted.dtype
    return pl.pallas_call(
        lambda *refs: reduce_kernel(n_vocab, *refs),
        name="reduce_to_owners",
        out_shape=jax.ShapeDtypeStruct((rows, quarter), kind),
        in_specs=[pl.BlockSpec(memory_space=pl.ANY)],
        out_specs=pl.BlockSpec(memory_space=pltpu.VMEM),
        scratch_shapes=[
            pltpu.VMEM((4, rows, width), kind),
            pltpu.VMEM((4, rows, width), kind),
            pltpu.VMEM((4, 2, rows, half), kind),
            pltpu.VMEM((2, rows, half), kind),
            pltpu.VMEM((2, rows, half), kind),
            pltpu.VMEM((rows, half), kind),
            pltpu.VMEM((rows, half), kind),
            pltpu.VMEM((n_vocab, rows, quarter), kind),
            pltpu.VMEM((n_vocab - 1, rows, quarter), kind),
            pltpu.SemaphoreType.DMA((9 + n_vocab,)),
            pltpu.SemaphoreType.DMA((9 + n_vocab,)),
            pltpu.SemaphoreType.DMA((4,)),
        ],
        compiler_params=pltpu.CompilerParams(
            collective_id=0, has_side_effects=True, vmem_limit_bytes=40 * 1024 * 1024),
    )(weighted.reshape(4, 2, rows, width))


def gather_kernel(n_vocab, rows_in, keys_in, every, keys, send, recv, local):
    me, z, core, x, y, sib, xn, yn, along_z, ids = peers_of(n_vocab)
    greet(ids)
    to_sib, to_x, to_y = ids[:3]
    across = xn + 4 - 8 * y
    started = []

    def move(src, dst, at, peer):
        return pltpu.make_async_remote_copy(
            src_ref=src, dst_ref=dst, send_sem=send.at[at], recv_sem=recv.at[at],
            device_id=peer, device_id_type=pl.DeviceIdType.MESH)

    def begin(src, dst, at, peer):
        moved = move(src, dst, at, peer)
        moved.start()
        started.append(moved)

    def arrived(ref, at):
        move(ref, ref, at, to_sib).wait_recv()

    far = n_vocab - 1
    base = 2 * far

    def number(kind, d):
        return base + kind * n_vocab + d

    for d in range(1, n_vocab):
        begin(rows_in, every.at[me, z], d - 1, {"vocab": along_z[d - 1]})
    own_rows = pltpu.make_async_copy(rows_in, every.at[me, z], local.at[0])
    own_keys = pltpu.make_async_copy(keys_in, keys.at[z], local.at[1])
    own_rows.start()
    own_keys.start()
    origin = [(z - d + n_vocab) % n_vocab for d in range(n_vocab)]
    for d in range(n_vocab):
        if d:
            arrived(every.at[me, origin[d]], d - 1)
        src = every.at[me, origin[d]] if d else rows_in
        begin(src, every.at[me, origin[d]], number(0, d), to_x)
        begin(src, every.at[me, origin[d]], number(1, d), to_y)
        begin(src, every.at[me, origin[d]], number(2, d), to_sib)
        if d == 0:
            for far_d in range(1, n_vocab):
                begin(keys_in, keys.at[z], far + far_d - 1, {"vocab": along_z[far_d - 1]})
    for d in range(n_vocab):
        arrived(every.at[xn, origin[d]], number(0, d))
        begin(every.at[xn, origin[d], 0], every.at[xn, origin[d], 0], number(3, d), to_y)
        begin(every.at[xn, origin[d]], every.at[xn, origin[d]], number(4, d), to_sib)
        arrived(every.at[yn, origin[d]], number(1, d))
        begin(every.at[yn, origin[d], 1], every.at[yn, origin[d], 1], number(5, d), to_x)
        begin(every.at[yn, origin[d]], every.at[yn, origin[d]], number(6, d), to_sib)
    for d in range(n_vocab):
        for h, kind in ((0, 3), (1, 5)):
            piece = every.at[across, origin[d], h]
            arrived(piece, number(kind, d))
            begin(piece, piece, number(7 + h, d), to_sib)
    sib_x, sib_y, sib_across = sib + 2 - 4 * x, sib + 4 - 8 * y, sib + 2 - 4 * x + 4 - 8 * y
    for d in range(n_vocab):
        arrived(every.at[sib, origin[d]], number(2, d))
        arrived(every.at[sib_x, origin[d]], number(4, d))
        arrived(every.at[sib_y, origin[d]], number(6, d))
        for h in range(2):
            arrived(every.at[sib_across, origin[d], h], number(7 + h, d))
        if d:
            arrived(keys.at[origin[d]], far + d - 1)
    own_rows.wait()
    own_keys.wait()
    for moved in started:
        moved.wait_send()


def gather_rows(expert_in, normed_rows, n_vocab):
    rows, width = expert_in.shape
    kind = expert_in.dtype
    count = 2 * (n_vocab - 1) + 9 * n_vocab
    every, keys = pl.pallas_call(
        lambda *refs: gather_kernel(n_vocab, *refs),
        name="gather_rows",
        out_shape=(
            jax.ShapeDtypeStruct((8, n_vocab, 2, rows // 2, width), kind),
            jax.ShapeDtypeStruct((n_vocab, rows, width), kind),
        ),
        in_specs=[pl.BlockSpec(memory_space=pl.ANY)] * 2,
        out_specs=(pl.BlockSpec(memory_space=pl.ANY), pl.BlockSpec(memory_space=pl.ANY)),
        scratch_shapes=[
            pltpu.SemaphoreType.DMA((count,)),
            pltpu.SemaphoreType.DMA((count,)),
            pltpu.SemaphoreType.DMA((2,)),
        ],
        compiler_params=pltpu.CompilerParams(collective_id=1, has_side_effects=True),
    )(expert_in.reshape(2, rows // 2, width), normed_rows)
    return every.reshape(8 * n_vocab * rows, width), keys.reshape(n_vocab * rows, width)


def on_device(
    token_ids,
    word_mask,
    embed_table,
    attn_out,
    in_gain,
    key_weight,
    key_gain,
    post_gain,
    routes,
    gate_ints,
    w_gate,
    w_up,
    w_down,
):
    n_vocab = lax.axis_size("vocab")
    n_expert = lax.axis_size("expert")
    vocab_rows = embed_table.shape[0]
    experts_total = n_expert * n_vocab // 2
    whole_mesh = ("expert", "vocab")
    by_kernel = n_expert == 8
    my_vocab = lax.axis_index("vocab")
    my_expert = (lax.axis_index("expert") * n_vocab + my_vocab) // 2

    gate_share = gate_ints.astype(jnp.float32) / jnp.sum(gate_ints, axis=1, keepdims=True).astype(
        jnp.float32
    )
    onehot = routes[:, :, None] == jnp.arange(experts_total, dtype=jnp.int32)[None, None, :]
    share_of = jnp.sum(jnp.where(onehot, gate_share[:, :, None], 0.0), axis=1)
    all_shares = lax.all_gather(share_of, "expert", axis=0, tiled=True)
    my_share = lax.dynamic_slice_in_dim(all_shares, my_expert, 1, axis=1)

    own_rows = attn_out.shape[0] // n_vocab
    attn_full = lax.all_gather(attn_out, "vocab", axis=1, tiled=True)
    attn_rows = lax.dynamic_slice_in_dim(attn_full, my_vocab * own_rows, own_rows, axis=0)

    local_ids = token_ids - my_vocab * vocab_rows
    inside = (local_ids >= 0) & (local_ids < vocab_rows)
    safe_ids = jnp.clip(local_ids, 0, vocab_rows - 1)
    keep_row = inside & (word_mask[safe_ids] == 1)
    partial_value = jnp.where(
        keep_row[:, None], embed_table[safe_ids], jnp.zeros_like(embed_table[:1])
    )
    moved_rows = lax.all_to_all(partial_value, "expert", split_axis=0, concat_axis=1, tiled=True)
    rows = lax.psum_scatter(moved_rows, "vocab", scatter_dimension=0, tiled=True)
    rows = rows.astype(jnp.float32)

    mid_rows = (rows + attn_rows.astype(jnp.float32)).astype(jnp.bfloat16)
    expert_in = rms_rows(mid_rows.astype(jnp.float32), post_gain).astype(jnp.bfloat16)
    normed_rows = rms_rows(rows, in_gain).astype(jnp.bfloat16)
    if by_kernel:
        tokens_in, key_rows = gather_rows(expert_in, normed_rows, n_vocab)
    else:
        tokens_in = lax.all_gather(expert_in, whole_mesh, axis=0, tiled=True)
        key_rows = lax.all_gather(normed_rows, "vocab", axis=0, tiled=True)
    raw_keys = jnp.dot(key_rows, key_weight, preferred_element_type=jnp.float32)
    key_heads = rms_rows(raw_keys, key_gain).astype(jnp.bfloat16)

    gate_val = jnp.dot(tokens_in, w_gate[0], preferred_element_type=jnp.float32)
    up_val = jnp.dot(tokens_in, w_up[0], preferred_element_type=jnp.float32)
    hidden = (jax.nn.silu(gate_val) * up_val).astype(jnp.bfloat16)
    parts = jnp.dot(hidden, w_down[0], preferred_element_type=jnp.float32)
    weighted = (parts * my_share).astype(jnp.bfloat16)
    if by_kernel:
        expert_out = reduce_to_owners(weighted, n_vocab)
    else:
        by_tokens = lax.psum_scatter(weighted, "expert", scatter_dimension=0, tiled=True)
        expert_out = lax.psum_scatter(by_tokens, "vocab", scatter_dimension=1, tiled=True)
    return (expert_out, key_heads)


def solution(mesh):
    return jax.shard_map(
        on_device,
        mesh=mesh,
        in_specs=(
            P(),
            P("vocab"),
            P("vocab", "expert"),
            P("expert", "vocab"),
            P(),
            P(None, "vocab"),
            P(),
            P(),
            P("expert", None),
            P("expert", None),
            P(("expert", "vocab"), None, None),
            P(("expert", "vocab"), None, None),
            P(("expert", "vocab"), None, None),
        ),
        out_specs=(P("expert", "vocab"), P("expert", "vocab")),
        check_vma=False,
    )
```

```python
import jax
import jax.numpy as jnp
from jax import lax
from jax.experimental import pallas as pl
from jax.experimental.pallas import tpu as pltpu
from jax.sharding import PartitionSpec as P


def rms_rows(values, scale_gain):
    inverse_rms = lax.rsqrt(jnp.mean(values * values, axis=-1, keepdims=True) + 1e-06)
    return values * inverse_rms * scale_gain


def greet(peers):
    barrier = pltpu.get_barrier_semaphore()
    for peer in peers:
        pl.semaphore_signal(barrier, inc=1, device_id=peer, device_id_type=pl.DeviceIdType.MESH)
    pl.semaphore_wait(barrier, len(peers))


def peers_of(n_vocab):
    me = lax.axis_index("expert")
    z = lax.axis_index("vocab")
    core, x, y = me % 2, (me // 2) % 2, me // 4
    sib, xn, yn = me + 1 - 2 * core, me + 2 - 4 * x, me + 4 - 8 * y
    along_z = [(z + d) % n_vocab for d in range(1, n_vocab)]
    ids = [{"expert": sib}, {"expert": xn}, {"expert": yn}] + [{"vocab": p} for p in along_z]
    return me, z, core, x, y, sib, xn, yn, along_z, ids


def add_rows(dst, terms):
    def step(i, carry):
        rows = pl.ds(pl.multiple_of(i * 16, 16), 16)
        total = terms[0][rows, :].astype(jnp.float32)
        for term in terms[1:]:
            total = total + term[rows, :].astype(jnp.float32)
        dst[rows, :] = total.astype(dst.dtype)
        return carry

    lax.fori_loop(0, dst.shape[0] // 16, step, 0)


def reduce_kernel(n_vocab, w, out, core_in, mine, held, a_in, b_in, a_last, b_last, full, z_in,
                  send, recv, local):
    me, z, core, x, y, sib, xn, yn, along_z, ids = peers_of(n_vocab)
    greet(ids)
    to_sib, to_x, to_y = ids[:3]
    chunk = [(1 - y) * 2 + 1 - x, y * 2 + 1 - x, (1 - y) * 2 + x, y * 2 + x]

    def move(src, dst, at, peer):
        return pltpu.make_async_remote_copy(
            src_ref=src, dst_ref=dst, send_sem=send.at[at], recv_sem=recv.at[at],
            device_id=peer, device_id_type=pl.DeviceIdType.MESH)

    core_moves = [move(w.at[chunk[r], 1 - core], core_in.at[r], r, to_sib) for r in range(4)]
    own = [pltpu.make_async_copy(w.at[chunk[r], core], mine.at[r], local.at[r]) for r in range(4)]
    for r in range(4):
        core_moves[r].start()
        own[r].start()
    a_moves = [move(held.at[0, 0], a_in.at[0], 4, to_x), move(held.at[1, 0], a_in.at[1], 5, to_x)]
    b_moves = [move(held.at[0, 1], b_in.at[0], 6, to_y), move(held.at[2, 1], b_in.at[1], 7, to_y)]
    a_then = move(held.at[2, 0], a_last, 8, to_y)
    b_then = move(held.at[1, 1], b_last, 9, to_x)
    half = held.shape[3]
    for r in range(4):
        own[r].wait()
        core_moves[r].wait_recv()
        for h in range(2):
            columns = pl.ds(h * half, half)
            add_rows(held.at[r, h], [mine.at[r, :, columns], core_in.at[r, :, columns]])
        if r == 0:
            a_moves[0].start()
            b_moves[0].start()
        if r == 1:
            a_moves[1].start()
        if r == 2:
            b_moves[1].start()
    a_moves[0].wait_recv()
    add_rows(held.at[2, 0], [held.at[2, 0], a_in.at[0]])
    a_then.start()
    b_moves[0].wait_recv()
    add_rows(held.at[1, 1], [held.at[1, 1], b_in.at[0]])
    b_then.start()
    quarter = full.shape[2]
    per_half = half // quarter
    for moves, then, came, last, h in ((a_moves, a_then, a_in, a_last, 0),
                                       (b_moves, b_then, b_in, b_last, 1)):
        moves[1].wait_recv()
        then.wait_recv()
        for q in range(per_half):
            columns = pl.ds(q * quarter, quarter)
            add_rows(full.at[h * per_half + q],
                     [held.at[3, h, :, columns], came.at[1, :, columns], last.at[:, columns]])
    z_moves = [move(full.at[along_z[d]], z_in.at[d], 10 + d, {"vocab": along_z[d]})
               for d in range(n_vocab - 1)]
    for moved in z_moves:
        moved.start()
    for moved in z_moves:
        moved.wait_recv()
    add_rows(out, [full.at[z]] + [z_in.at[d] for d in range(n_vocab - 1)])
    for moved in core_moves + a_moves + b_moves + [a_then, b_then] + z_moves:
        moved.wait_send()


def reduce_to_owners(weighted, n_vocab):
    tokens, width = weighted.shape
    rows, half, quarter = tokens // 8, width // 2, width // n_vocab
    kind = weighted.dtype
    return pl.pallas_call(
        lambda *refs: reduce_kernel(n_vocab, *refs),
        name="reduce_to_owners",
        out_shape=jax.ShapeDtypeStruct((rows, quarter), kind),
        in_specs=[pl.BlockSpec(memory_space=pl.ANY)],
        out_specs=pl.BlockSpec(memory_space=pltpu.VMEM),
        scratch_shapes=[
            pltpu.VMEM((4, rows, width), kind),
            pltpu.VMEM((4, rows, width), kind),
            pltpu.VMEM((4, 2, rows, half), kind),
            pltpu.VMEM((2, rows, half), kind),
            pltpu.VMEM((2, rows, half), kind),
            pltpu.VMEM((rows, half), kind),
            pltpu.VMEM((rows, half), kind),
            pltpu.VMEM((n_vocab, rows, quarter), kind),
            pltpu.VMEM((n_vocab - 1, rows, quarter), kind),
            pltpu.SemaphoreType.DMA((9 + n_vocab,)),
            pltpu.SemaphoreType.DMA((9 + n_vocab,)),
            pltpu.SemaphoreType.DMA((4,)),
        ],
        compiler_params=pltpu.CompilerParams(
            collective_id=0, has_side_effects=True, vmem_limit_bytes=40 * 1024 * 1024),
    )(weighted.reshape(4, 2, rows, width))


def gather_kernel(n_vocab, rows_in, keys_in, every, keys, send, recv, local):
    me, z, core, x, y, sib, xn, yn, along_z, ids = peers_of(n_vocab)
    greet(ids)
    to_sib, to_x, to_y = ids[:3]
    across = xn + 4 - 8 * y
    started = []

    def move(src, dst, at, peer):
        return pltpu.make_async_remote_copy(
            src_ref=src, dst_ref=dst, send_sem=send.at[at], recv_sem=recv.at[at],
            device_id=peer, device_id_type=pl.DeviceIdType.MESH)

    def begin(src, dst, at, peer):
        moved = move(src, dst, at, peer)
        moved.start()
        started.append(moved)

    def arrived(ref, at):
        move(ref, ref, at, to_sib).wait_recv()

    far = n_vocab - 1
    base = 2 * far

    def number(kind, d):
        return base + kind * n_vocab + d

    for d in range(1, n_vocab):
        begin(rows_in, every.at[me, z], d - 1, {"vocab": along_z[d - 1]})
    own_rows = pltpu.make_async_copy(rows_in, every.at[me, z], local.at[0])
    own_keys = pltpu.make_async_copy(keys_in, keys.at[z], local.at[1])
    own_rows.start()
    own_keys.start()
    origin = [(z - d + n_vocab) % n_vocab for d in range(n_vocab)]
    for d in range(n_vocab):
        if d:
            arrived(every.at[me, origin[d]], d - 1)
        src = every.at[me, origin[d]] if d else rows_in
        begin(src, every.at[me, origin[d]], number(0, d), to_x)
        begin(src, every.at[me, origin[d]], number(1, d), to_y)
        begin(src, every.at[me, origin[d]], number(2, d), to_sib)
        if d == 0:
            for far_d in range(1, n_vocab):
                begin(keys_in, keys.at[z], far + far_d - 1, {"vocab": along_z[far_d - 1]})
    for d in range(n_vocab):
        arrived(every.at[xn, origin[d]], number(0, d))
        begin(every.at[xn, origin[d], 0], every.at[xn, origin[d], 0], number(3, d), to_y)
        begin(every.at[xn, origin[d]], every.at[xn, origin[d]], number(4, d), to_sib)
        arrived(every.at[yn, origin[d]], number(1, d))
        begin(every.at[yn, origin[d], 1], every.at[yn, origin[d], 1], number(5, d), to_x)
        begin(every.at[yn, origin[d]], every.at[yn, origin[d]], number(6, d), to_sib)
    for d in range(n_vocab):
        for h, kind in ((0, 3), (1, 5)):
            piece = every.at[across, origin[d], h]
            arrived(piece, number(kind, d))
            begin(piece, piece, number(7 + h, d), to_sib)
    sib_x, sib_y, sib_across = sib + 2 - 4 * x, sib + 4 - 8 * y, sib + 2 - 4 * x + 4 - 8 * y
    for d in range(n_vocab):
        arrived(every.at[sib, origin[d]], number(2, d))
        arrived(every.at[sib_x, origin[d]], number(4, d))
        arrived(every.at[sib_y, origin[d]], number(6, d))
        for h in range(2):
            arrived(every.at[sib_across, origin[d], h], number(7 + h, d))
        if d:
            arrived(keys.at[origin[d]], far + d - 1)
    own_rows.wait()
    own_keys.wait()
    for moved in started:
        moved.wait_send()


def gather_rows(expert_in, normed_rows, n_vocab):
    rows, width = expert_in.shape
    kind = expert_in.dtype
    count = 2 * (n_vocab - 1) + 9 * n_vocab
    every, keys = pl.pallas_call(
        lambda *refs: gather_kernel(n_vocab, *refs),
        name="gather_rows",
        out_shape=(
            jax.ShapeDtypeStruct((8, n_vocab, 2, rows // 2, width), kind),
            jax.ShapeDtypeStruct((n_vocab, rows, width), kind),
        ),
        in_specs=[pl.BlockSpec(memory_space=pl.ANY)] * 2,
        out_specs=(pl.BlockSpec(memory_space=pl.ANY), pl.BlockSpec(memory_space=pl.ANY)),
        scratch_shapes=[
            pltpu.SemaphoreType.DMA((count,)),
            pltpu.SemaphoreType.DMA((count,)),
            pltpu.SemaphoreType.DMA((2,)),
        ],
        compiler_params=pltpu.CompilerParams(collective_id=1, has_side_effects=True),
    )(expert_in.reshape(2, rows // 2, width), normed_rows)
    return every.reshape(8 * n_vocab * rows, width), keys.reshape(n_vocab * rows, width)


def on_device(
    token_ids,
    word_mask,
    embed_table,
    attn_out,
    in_gain,
    key_weight,
    key_gain,
    post_gain,
    routes,
    gate_ints,
    w_gate,
    w_up,
    w_down,
):
    n_vocab = lax.axis_size("vocab")
    n_expert = lax.axis_size("expert")
    vocab_rows = embed_table.shape[0]
    experts_total = n_expert * n_vocab // 2
    whole_mesh = ("expert", "vocab")
    by_kernel = n_expert == 8
    my_vocab = lax.axis_index("vocab")
    my_expert = (lax.axis_index("expert") * n_vocab + my_vocab) // 2

    gate_share = gate_ints.astype(jnp.float32) / jnp.sum(gate_ints, axis=1, keepdims=True).astype(
        jnp.float32
    )
    onehot = routes[:, :, None] == jnp.arange(experts_total, dtype=jnp.int32)[None, None, :]
    share_of = jnp.sum(jnp.where(onehot, gate_share[:, :, None], 0.0), axis=1)
    all_shares = lax.all_gather(share_of, "expert", axis=0, tiled=True)
    my_share = lax.dynamic_slice_in_dim(all_shares, my_expert, 1, axis=1)

    own_rows = attn_out.shape[0] // n_vocab
    attn_blocks = attn_out.reshape(n_vocab, own_rows, attn_out.shape[1])
    kept = lax.dynamic_index_in_dim(attn_blocks, my_vocab, 0, keepdims=True)
    attn_parts = lax.dynamic_update_slice_in_dim(attn_blocks, kept, my_vocab, 0)
    for d in range(1, n_vocab):
        sent = lax.dynamic_index_in_dim(attn_blocks, (my_vocab + d) % n_vocab, 0, keepdims=True)
        came = lax.ppermute(sent, "vocab", [(i, (i + d) % n_vocab) for i in range(n_vocab)])
        attn_parts = lax.dynamic_update_slice_in_dim(
            attn_parts, came, (my_vocab - d + n_vocab) % n_vocab, 0
        )
    attn_rows = attn_parts.transpose(1, 0, 2).reshape(own_rows, -1)

    ids = token_ids.reshape(n_expert, n_vocab, own_rows).transpose(1, 0, 2).reshape(-1)
    local_ids = ids - my_vocab * vocab_rows
    inside = (local_ids >= 0) & (local_ids < vocab_rows)
    safe_ids = jnp.clip(local_ids, 0, vocab_rows - 1)
    keep_row = inside & (word_mask[safe_ids] == 1)
    partial_value = jnp.where(
        keep_row[:, None], embed_table[safe_ids], jnp.zeros_like(embed_table[:1])
    )
    summed = lax.psum_scatter(partial_value, "vocab", scatter_dimension=0, tiled=True)
    rows = lax.all_to_all(summed, "expert", split_axis=0, concat_axis=1, tiled=True)
    rows = rows.astype(jnp.float32)

    mid_rows = (rows + attn_rows.astype(jnp.float32)).astype(jnp.bfloat16)
    expert_in = rms_rows(mid_rows.astype(jnp.float32), post_gain).astype(jnp.bfloat16)
    normed_rows = rms_rows(rows, in_gain).astype(jnp.bfloat16)
    if by_kernel:
        tokens_in, key_rows = gather_rows(expert_in, normed_rows, n_vocab)
    else:
        tokens_in = lax.all_gather(expert_in, whole_mesh, axis=0, tiled=True)
        key_rows = lax.all_gather(normed_rows, "vocab", axis=0, tiled=True)
    raw_keys = jnp.dot(key_rows, key_weight, preferred_element_type=jnp.float32)
    key_heads = rms_rows(raw_keys, key_gain).astype(jnp.bfloat16)

    gate_val = jnp.dot(tokens_in, w_gate[0], preferred_element_type=jnp.float32)
    up_val = jnp.dot(tokens_in, w_up[0], preferred_element_type=jnp.float32)
    hidden = (jax.nn.silu(gate_val) * up_val).astype(jnp.bfloat16)
    parts = jnp.dot(hidden, w_down[0], preferred_element_type=jnp.float32)
    weighted = (parts * my_share).astype(jnp.bfloat16)
    if by_kernel:
        expert_out = reduce_to_owners(weighted, n_vocab)
    else:
        by_tokens = lax.psum_scatter(weighted, "expert", scatter_dimension=0, tiled=True)
        expert_out = lax.psum_scatter(by_tokens, "vocab", scatter_dimension=1, tiled=True)
    return (expert_out, key_heads)


def solution(mesh):
    return jax.shard_map(
        on_device,
        mesh=mesh,
        in_specs=(
            P(),
            P("vocab"),
            P("vocab", "expert"),
            P("expert", "vocab"),
            P(),
            P(None, "vocab"),
            P(),
            P(),
            P("expert", None),
            P("expert", None),
            P(("expert", "vocab"), None, None),
            P(("expert", "vocab"), None, None),
            P(("expert", "vocab"), None, None),
        ),
        out_specs=(P("expert", "vocab"), P("expert", "vocab")),
        check_vma=False,
    )
```
